1024 devices in a mesh: rep: 8 (over x_lo, core), col: 128 (over x_hi, y, z).
Axes of the slice: x: 8 (x_hi: 2, x_lo: 4; x = x_hi * 4 + x_lo), y: 8, z: 8, core: 2. Of those that a mesh axis runs over, the one named last changes fastest.
Arguments:
- tokens_learn: bfloat16 [5120, 2048], P(None, 'rep'), may hold values from -6 to 6
- cotangent: bfloat16 [2048, 27648], P('rep', 'col'), may hold values from -6 to 6
- sample_ids: int32 [8, 256], P('rep'), may hold values from 0 to 7, never falling along the last dimension, each value on 1 to 64 neighbouring positions
- advantage: float32 [8, 8], P('rep'), may hold values from -2 to 2
- up_weight: bfloat16 [5120, 27648], P('rep', 'col'), may hold values from -0.078125 to 0.078125
- first_moment: float32 [5120, 27648], P('rep', 'col'), may hold values from -3 to 3
- second_moment: float32 [5120, 27648], P('rep', 'col'), may hold values from 0.05 to 1
- rollout_rows: bfloat16 [1024, 5120], P('rep', 'col'), may hold values from -6 to 6
- down_proj: bfloat16 [5120, 27648], P(None, 'col'), may hold values from -0.0390625 to 0.0390625
- live_lengths: int32 [8, 4], P('rep'), may hold values from 1 to 32, 96 in all within a row
Outputs:
- new_weight: bfloat16 [5120, 27648], P('rep', 'col')
- new_first: float32 [5120, 27648], P('rep', 'col')
- new_second: float32 [5120, 27648], P('rep', 'col')
- rollout_out: bfloat16 [5120, 1024], P('col', 'rep')
The draws below stay inside these ranges and needn't reach their ends.
Inputs may be any that keep to these rules, and one draw needn't show every extreme that they name: `sample_ids`: each lane's sample ids never fall along the lane, and each of the 8 samples has 1 to 64 tokens of that lane. `live_lengths`: the 4 lengths of a replica sum to 96, and one of them is 32.
All inputs are finite; a program needn't handle non-finite values.
Results may differ from the reference program's by a relative error of at most 0.019.
Values may be sent and summed in bfloat16 or wider, within the bound.
A program may use at most 64 MiB of HBM per device.

```python
import math
import jax
import jax.numpy as jnp
import numpy as np
from jax import lax

D = 5120
FF = 27648
TOK_DEV = 256
SAMPLES = 8
SEG_MOST = 64
SEQS = 4
SLOT = 32
ROWS = 128
LIVE = 96
LANES = 8
REPLICAS = 8


def strengthened(result, stream_key, source, target, parts, factor):
    def block_of(position):
        return (jnp.arange(result.shape[position]) // (result.shape[position] // parts)).reshape((-1,) + (1,) * (result.ndim - 1 - position))

    near = jax.random.permutation(stream_key, parts)[block_of(target)]
    other_side = (block_of(target) + parts // 2) % parts
    return jnp.where((block_of(source) == near) | (block_of(source) == other_side), factor * result, result)


def shard_levels(key, dims, split, low, largest):
    factor_of = 1.0
    for position, blocks in split:
        heights = jax.random.uniform(jax.random.fold_in(jax.random.fold_in(key, 6), position), (blocks,), jnp.float32, low / len(split), largest / len(split))
        factor_of = factor_of * jnp.repeat(jnp.exp(heights), dims[position] // blocks).reshape((-1,) + (1,) * (len(dims) - 1 - position))
    return factor_of


def split_up(count, total, reach, slope):
    loads = [(1 << 20) // math.isqrt(grade ** slope) + 1 for grade in range(2, count + 1)]
    surplus, holding = total - reach - (count - 1), [1] * (count - 1)
    while surplus > 0:
        free = [i for i in range(count - 1) if holding[i] < reach]
        mass, remaining = sum([loads[i] for i in free]), surplus
        for i in free:
            addition = min(reach - holding[i], max(1, remaining * loads[i] // mass), surplus)
            holding[i] = holding[i] + addition
            surplus = surplus - addition
    return np.array([reach] + holding)


def uneven(key, number_of, total, limit, slope):
    if number_of == 2:
        one = jax.random.randint(key, (), max(1, total - limit), min(limit, total - 1) + 1)
        return jnp.stack([one, total - one])
    sizes = jnp.asarray(split_up(number_of, total, limit, slope), jnp.int32)
    twos = (number_of - 1) // 2
    donor, receiver = sizes[1:1 + 2 * twos:2], sizes[2:2 + 2 * twos:2]
    slack = jnp.minimum(donor - 1, limit - receiver)
    shifted = jax.random.randint(jax.random.fold_in(key, 1), (twos,), 0, 1 << 20) % (slack + 1)
    sizes = sizes.at[1:1 + 2 * twos:2].set(donor - shifted).at[2:2 + 2 * twos:2].set(receiver + shifted)
    return sizes[jax.random.permutation(jax.random.fold_in(key, 2), number_of)]


def centred(own_key, extent, scale, bound, cuts=(), kind=jnp.bfloat16):
    entries = jax.random.normal(own_key, extent, jnp.float32) * scale
    if len(cuts) > 0:
        entries = shard_levels(own_key, extent, cuts, -0.22, 0.18) * entries
    return jnp.clip(entries, min=-bound, max=bound).astype(kind)


def gaussian_with(own_key, extent, spread, most, split, heavy, kind=jnp.bfloat16):
    array = spread * jax.random.normal(own_key, extent, jnp.float32)
    if split:
        array = array * shard_levels(own_key, extent, split, -0.22, 0.18)
    return jnp.clip(strengthened(array, jax.random.fold_in(own_key, 3), *heavy), -most, most).astype(kind)


def setup_inputs(seed: int = 0) -> dict:
    key_list = jax.random.split(jax.random.key(seed), 11)
    tokens_learn = gaussian_with(key_list[0], (D, LANES * TOK_DEV), 1.0, 6.0, ((1, 8),), (1, 0, 8, 2.0))
    cotangent = centred(key_list[1], (LANES * TOK_DEV, FF), 1.0, 6.0, ((0, 8), (1, 128)))
    sample_ids = jax.vmap(lambda own: jnp.searchsorted(jnp.cumsum(uneven(own, SAMPLES, TOK_DEV, SEG_MOST, 1)), jnp.arange(TOK_DEV), side="right"))(jax.random.split(key_list[2], LANES)).reshape((LANES, TOK_DEV)).astype(jnp.int32)
    advantage = jnp.clip(jax.random.uniform(key_list[3], (LANES, SAMPLES), jnp.float32, -2.0, 2.0) * shard_levels(key_list[3], (LANES, SAMPLES), ((0, 8),), -0.4, 0.0), -2.0, 2.0)
    up_weight = centred(key_list[4], (D, FF), D ** -0.5, 0.078125, ((0, 8), (1, 128)))
    first_moment = centred(key_list[5], (D, FF), 0.3, 3.0, ((0, 8), (1, 128)), jnp.float32)
    second_moment = jnp.clip(jnp.exp(math.log(1.0) - 2.9957323 * jax.random.uniform(key_list[6], (D, FF), jnp.float32) ** shard_levels(key_list[6], (D, FF), ((0, 8), (1, 128)), -0.2, 0.2)), 0.05, 1.0)
    rollout_rows = centred(key_list[7], (REPLICAS * ROWS, D), 1.0, 6.0, ((0, 8), (1, 128)))
    down_proj = centred(key_list[8], (D, FF), FF ** -0.5, 0.0390625, ((1, 128),))
    live_lengths = jax.vmap(lambda own: uneven(own, SEQS, LIVE, SLOT, 1))(jax.random.split(key_list[9], REPLICAS)).reshape((REPLICAS, SEQS)).astype(jnp.int32)
    return {"tokens_learn": tokens_learn, "cotangent": cotangent, "sample_ids": sample_ids, "advantage": advantage, "up_weight": up_weight, "first_moment": first_moment, "second_moment": second_moment, "rollout_rows": rollout_rows, "down_proj": down_proj, "live_lengths": live_lengths}


first_decay = 0.9
second_decay = 0.95
learn_rate = 0.003
decay_weight = 0.1
adam_epsilon = 1e-08
first_bias = 1.0 - math.exp(100.0 * math.log(0.9))
second_bias = 1.0 - math.exp(100.0 * math.log(0.95))

def token_scales(sample_ids, advantage):
    members = (sample_ids[..., :, None] == jnp.arange(advantage.shape[-1], dtype=jnp.int32)).astype(jnp.float32)
    counts = lax.optimization_barrier(jnp.sum(members, axis=-2))
    ratios = advantage / counts
    return lax.optimization_barrier(jnp.sum(members * ratios[..., None, :], axis=-1))

def adam_update(gradient, up_weight, first_moment, second_moment):
    new_first = first_decay * first_moment + (1.0 - first_decay) * gradient
    new_second = second_decay * second_moment + (1.0 - second_decay) * gradient * gradient
    direction = new_first / first_bias / (jnp.sqrt(new_second / second_bias) + adam_epsilon)
    weight_wide = up_weight.astype(jnp.float32)
    new_weight = (weight_wide - learn_rate * (direction + decay_weight * weight_wide)).astype(jnp.bfloat16)
    return (new_weight, new_first, new_second)

def live_rows(live_lengths, rows_each):
    slot_len = rows_each // SEQS
    positions = jnp.arange(rows_each, dtype=jnp.int32)
    which = positions // slot_len
    within = positions % slot_len
    picks = (which[:, None] == jnp.arange(SEQS, dtype=jnp.int32)[None, :]).astype(jnp.int32)
    limits = lax.optimization_barrier(jnp.sum(live_lengths[:, None, :] * picks[None, :, :], axis=-1))
    return (within[None, :] < limits).astype(jnp.float32).reshape(-1)

def wide_dot(left, right):
    return jnp.dot(left.astype(jnp.float32), right.astype(jnp.float32), precision=lax.Precision.HIGHEST, preferred_element_type=jnp.float32)

def reference(tokens_learn, cotangent, sample_ids, advantage, up_weight, first_moment, second_moment, rollout_rows, down_proj, live_lengths):
    lane_count = advantage.shape[0]
    token_scale = token_scales(sample_ids, advantage)
    token_blocks = jnp.transpose(tokens_learn.reshape(D, lane_count, TOK_DEV), (1, 0, 2))
    cotan_blocks = cotangent.reshape(lane_count, TOK_DEV, FF)

    def lane_step(running, lane_items):
        lane_tokens, lane_cotan, lane_scale = lane_items
        scaled = (lane_scale[:, None] * lane_cotan.astype(jnp.float32)).astype(jnp.bfloat16)
        partial_value = wide_dot(lane_tokens, scaled).astype(jnp.bfloat16)
        return (running + partial_value.astype(jnp.float32), None)
    gradient, _ = lax.scan(lane_step, jnp.zeros((D, FF), jnp.float32), (token_blocks, cotan_blocks, token_scale))
    new_weight, new_first, new_second = adam_update(gradient, up_weight, first_moment, second_moment)
    pre_act = wide_dot(rollout_rows, new_weight)
    live_mask = live_rows(live_lengths, ROWS)
    activation = (jax.nn.silu(pre_act) * live_mask[:, None]).astype(jnp.bfloat16)
    rollout_out = wide_dot(down_proj, activation.T).astype(jnp.bfloat16)
    return (new_weight, new_first, new_second, rollout_out)
```

```python
import math

import jax
import jax.numpy as jnp
from jax import lax
from jax.experimental import pallas as pl
from jax.experimental.pallas import tpu as pltpu
from jax.sharding import Mesh
from jax.sharding import PartitionSpec as P

SEQS = 4
REP = ("rep_0", "rep_1")
COL = ("col_0", "col_1", "col_2")
Q, K, XH, Y, Z = "rep_0", "rep_1", "col_0", "col_1", "col_2"
MESH = pl.DeviceIdType.MESH
F32 = jnp.float32
BF16 = jnp.bfloat16

first_decay = 0.9
second_decay = 0.95
learn_rate = 0.003
decay_weight = 0.1
adam_epsilon = 1e-08
first_bias = 1.0 - math.exp(100.0 * math.log(0.9))
second_bias = 1.0 - math.exp(100.0 * math.log(0.95))

BLK = 640
COLS = 216
TOK = 256
ROWS = 128
FEAT = 40
HALF = 320
PIECES = ((0, 64), (64, 64), (128, 48), (176, 40))
RING = (4, 3, 5, 2, 6, 1, 7)

S_TOK, S_SC, S_R, S_L, S_X1 = 0, 4, 5, 21, 37
S_2A, S_2B, S_3A, S_3B, S_PRE = 39, 47, 55, 63, 71
S_1DA, S_1DB, S_2DA, S_2DB, S_XH = 79, 87, 95, 103, 111
N_SEM = 112
L_TOK, L_W, L_M, L_V, L_DN, L_OUT = 0, 4, 5, 6, 7, 8
N_LOCAL = 11


def adam_update(gradient, up_weight, first_moment, second_moment):
    new_first = first_decay * first_moment + (1.0 - first_decay) * gradient
    new_second = second_decay * second_moment + (1.0 - second_decay) * gradient * gradient
    direction = new_first / first_bias / (jnp.sqrt(new_second / second_bias) + adam_epsilon)
    weight_wide = up_weight.astype(F32)
    new_weight = (weight_wide - learn_rate * (direction + decay_weight * weight_wide)).astype(BF16)
    return (new_weight, new_first, new_second)


def kernel(
    tok, cot, ids, adv, lens, w_in, m_in, v_in, x_in, down,
    w_out, m_out, v_out, o_out,
    tok_a, tok_b, sc_o, sc_p, part, r_in, l_in, r_send, l_send,
    gath, p_send, p_recv,
    w_s, m_s, v_s, w_n, m_n, v_n, dn, dn_t, of,
    a_send, a_recv, b_send, b_recv, own_a, sum_a, sum_b,
    a2_send, a2_recv, b2_send, b2_recv, x_send, x_recv,
    send, recv, local,
):
    q, k = lax.axis_index(Q), lax.axis_index(K)
    xh, y, z = lax.axis_index(XH), lax.axis_index(Y), lax.axis_index(Z)
    r = 2 * q + k

    def remote(src, dst, at_send, at_recv, where):
        return pltpu.make_async_remote_copy(
            src_ref=src,
            dst_ref=dst,
            send_sem=send.at[at_send],
            recv_sem=recv.at[at_recv],
            device_id=where,
            device_id_type=MESH,
        )

    leaving = []

    def send_to(src, dst, at_send, at_recv, where):
        copy = remote(src, dst, at_send, at_recv, where)
        copy.start()
        leaving.append(copy.wait_send)

    def arrived(dst, at_recv):
        remote(dst, dst, 0, at_recv, {K: 1 - k}).wait_recv()

    def sent(src, at_send):
        remote(src, src, at_send, 0, {K: 1 - k}).wait_send()

    barrier = pltpu.get_barrier_semaphore()

    def greet(where):
        pl.semaphore_signal(barrier, inc=1, device_id=where, device_id_type=MESH)

    from_q, from_k, from_x = y // 2, y % 2, q // 2
    from_y = [4 * (q % 2) + 2 * k + j for j in range(2)]
    mine_from = [(from_q == q) & (from_k == k) & (from_x == xh) & (from_y[j] == y) for j in range(2)]
    to_q, to_k = 2 * xh + y // 4, (y // 2) % 2
    mine_to = [(to_q == q) & (to_k == k) & (xh == h) & (r == y) for h in range(2)]

    for d in range(1, 8):
        other = (r + d) % 8
        greet({Q: other // 2, K: other % 2})
        greet({Y: (y + d) % 8})
        greet({Z: (z + d) % 8})
    greet({XH: 1 - xh})
    for j in range(2):

        @pl.when(jnp.logical_not(mine_from[j]))
        def _():
            greet({Q: from_q, K: from_k, XH: from_x, Y: from_y[j], Z: z})

    def block_rows(b, parity):
        return pl.ds(pl.multiple_of((2 * b + parity) * BLK, BLK), BLK)

    order = (3, 0, 2, 1)
    loads = [pltpu.make_async_copy(tok.at[block_rows(b, k)], tok_a.at[b], local.at[L_TOK + b]) for b in range(4)]
    for b in order:
        loads[b].start()
    late = [
        pltpu.make_async_copy(w_in, w_s, local.at[L_W]),
        pltpu.make_async_copy(m_in, m_s, local.at[L_M]),
        pltpu.make_async_copy(v_in, v_s, local.at[L_V]),
        pltpu.make_async_copy(down, dn, local.at[L_DN]),
    ]
    for copy in late:
        copy.start()

    sample = lax.broadcasted_iota(jnp.int32, (8, TOK), 0)
    members = (ids[...] == sample).astype(F32)
    counts = jnp.sum(members, axis=1, keepdims=True)
    eye = lax.broadcasted_iota(jnp.int32, (8, 8), 0) == lax.broadcasted_iota(jnp.int32, (8, 8), 1)
    tall = jnp.sum(jnp.where(eye, adv[...], 0.0), axis=1, keepdims=True)
    scale = jnp.sum(members * (tall / counts), axis=0, keepdims=True)
    sc_o[...] = (scale * cot[...].astype(F32)).astype(BF16)

    pl.semaphore_wait(barrier, 24 - mine_to[0].astype(jnp.int32) - mine_to[1].astype(jnp.int32))

    for h in range(2):

        @pl.when(jnp.logical_not(mine_to[h]))
        def _():
            remote(x_in, gath.at[r, y % 2, z], S_X1 + h, S_X1 + y % 2, {Q: to_q, K: to_k, XH: h, Y: r, Z: z}).start()

        @pl.when(mine_to[h])
        def _():
            gath[r, y % 2, z] = x_in[...]

    send_to(sc_o, sc_p, S_SC, S_SC, {K: 1 - k})
    for b in order:
        send_to(tok.at[block_rows(b, 1 - k)], tok_b.at[b], S_TOK + b, S_TOK + b, {K: 1 - k})

    def running(b, s, first, sums, out, at, target):
        rows = pl.ds(*PIECES[s])
        value = part[b, rows]
        if not first:
            arrived(sums.at[b, rows], at + 4 * b + s)
            value = value + sums[b, rows].astype(F32)
        out[b, rows] = value.astype(BF16)
        remote(out.at[b, rows], sums.at[b, rows], at + 4 * b + s, at + 4 * b + s, {Q: target}).start()

    def right(b, s, first):
        running(b, s, first, r_in, r_send, S_R, q + 1)

    def left(b, s, first):
        running(b, s, first, l_in, l_send, S_L, q - 1)

    def over_tokens(scaled, tokens):
        return lax.dot_general(scaled, tokens, (((1,), (1,)), ((), ())), preferred_element_type=F32)

    arrived(sc_p, S_SC)
    for b in order:
        loads[b].wait()
        arrived(tok_b.at[b], S_TOK + b)

        part[b] = over_tokens(sc_o[...], tok_a[b]) + over_tokens(sc_p[...], tok_b[b])

        if b > 0:

            @pl.when(q == 0)
            def _():
                for s in range(4):
                    right(b, s, True)

        if b < 3:

            @pl.when(q == 3)
            def _():
                for s in range(4):
                    left(b, s, True)

    for j in range(2):

        @pl.when(jnp.logical_not(mine_from[j]))
        def _():
            arrived(gath.at[y, j, z], S_X1 + j)

    for d in RING:
        oz, oy = (z + d) % 8, (y + d) % 8
        here = gath.at[y, 0, z]
        send_to(here, here, S_2A + oz, S_2A + z, {Z: oz})
        here = gath.at[y, 1, z]
        send_to(here, here, S_2B + oy, S_2B + y, {Y: oy})

    @pl.when((q > 0) & (q < 3))
    def _():
        for s in range(4):
            right(3, s, False)
            left(0, s, False)

    for d in reversed(RING):
        oz = (z + d) % 8
        arrived(gath.at[y, 0, oz], S_2A + oz)
    for d in RING:
        oy = (y + d) % 8
        here = gath.at[y, 0]
        send_to(here, here, S_3A + oy, S_3A + y, {Y: oy})
    for d in reversed(RING):
        oy = (y + d) % 8
        arrived(gath.at[oy, 1, z], S_2B + oy)
    for d in RING:
        oz = (z + d) % 8
        here = gath.at[:, 1, z]
        send_to(here, here, S_3B + oz, S_3B + z, {Z: oz})

    @pl.when(q == 1)
    def _():
        for s in range(4):
            right(2, s, False)

    @pl.when(q == 2)
    def _():
        for s in range(4):
            left(1, s, False)

    late[3].wait()

    @pl.loop(0, 8)
    def _(i):
        at = pl.ds(pl.multiple_of(i * BLK, BLK), BLK)
        wide = jnp.concatenate([dn[:, at].astype(F32), jnp.zeros((256 - COLS, BLK), F32)], axis=0)
        dn_t[at] = jnp.transpose(wide)[:, :COLS].astype(BF16)

    @pl.when(q > 0)
    def _():
        for s in range(4):
            arrived(r_in.at[q, pl.ds(*PIECES[s])], S_R + 4 * q + s)

    @pl.when(q < 3)
    def _():
        for s in range(4):
            arrived(l_in.at[q, pl.ds(*PIECES[s])], S_L + 4 * q + s)

    for copy in late[:3]:
        copy.wait()
    has_left, has_right = q > 0, q < 3

    @pl.loop(0, 5)
    def _(i):
        lanes = pl.ds(pl.multiple_of(i * 128, 128), 128)
        for piece in PIECES:
            rows = pl.ds(*piece)
            gradient = part[q, rows, lanes]
            gradient = gradient + jnp.where(has_left, r_in[q, rows, lanes].astype(F32), 0.0)
            gradient = gradient + jnp.where(has_right, l_in[q, rows, lanes].astype(F32), 0.0)
            new = adam_update(gradient, w_s[rows, lanes], m_s[rows, lanes], v_s[rows, lanes])
            w_n[rows, lanes], m_n[rows, lanes], v_n[rows, lanes] = new

    outs = [
        pltpu.make_async_copy(w_n, w_out, local.at[L_OUT]),
        pltpu.make_async_copy(m_n, m_out, local.at[L_OUT + 1]),
        pltpu.make_async_copy(v_n, v_out, local.at[L_OUT + 2]),
    ]
    for copy in outs:
        copy.start()
        leaving.append(copy.wait)

    for d in RING:
        oy, oz = (y + d) % 8, (z + d) % 8
        arrived(gath.at[oy, 0], S_3A + oy)
        arrived(gath.at[:, 1, oz], S_3B + oz)

    def partial_of(other):
        return jnp.dot(w_n[...], gath[other].reshape(BLK, ROWS), preferred_element_type=F32)

    for d in (7, 6, 5, 4, 3, 2, 1):
        other = (r + d) % 8
        p_send[other] = partial_of(other).astype(BF16)
        send_to(p_send.at[other], p_recv.at[r], S_PRE + other, S_PRE + r, {Q: other // 2, K: other % 2})
    pre = partial_of(r)
    for d in range(1, 8):
        other = (r + d) % 8
        arrived(p_recv.at[other], S_PRE + other)
        pre = pre + p_recv[other].astype(F32)

    lane = lax.broadcasted_iota(jnp.int32, (1, ROWS), 1)
    slot_len = ROWS // SEQS
    limit = jnp.zeros((1, ROWS), jnp.int32)
    for s in range(SEQS):
        limit = jnp.where(lane // slot_len == s, lens[0, s], limit)
    live = lane % slot_len < limit
    act = jnp.where(live, pre / (1.0 + jnp.exp(-pre)), 0.0).astype(BF16)

    for n, d in enumerate(RING + (0,)):
        oy = (y + d) % 8
        rows = pl.ds(pl.multiple_of(oy * HALF, HALF), HALF)
        value = jnp.dot(dn_t[rows], act, preferred_element_type=F32)
        if d == 0:
            own_a[...] = value
        else:
            a_send[oy] = value.astype(BF16)
            send_to(a_send.at[oy], a_recv.at[y], S_1DA + oy, S_1DA + y, {Y: oy})
        of[pl.ds(n * HALF, HALF)] = jnp.dot(
            dn_t[pl.ds(8 * HALF + n * HALF, HALF)], act, preferred_element_type=F32
        )

    def turned(oz):
        return jnp.concatenate(
            [of[pl.ds(pl.multiple_of(i * HALF + oz * FEAT, 8), FEAT)] for i in range(8)], axis=0
        )

    for d in RING:
        oz = (z + d) % 8
        b_send[oz] = turned(oz).astype(BF16)
        send_to(b_send.at[oz], b_recv.at[z], S_1DB + oz, S_1DB + z, {Z: oz})

    value = own_a[...]
    for d in RING:
        oy = (y + d) % 8
        arrived(a_recv.at[oy], S_1DA + oy)
        value = value + a_recv[oy].astype(F32)
    sum_a[...] = value
    for d in RING:
        oz = (z + d) % 8
        a2_send[oz] = sum_a[pl.ds(pl.multiple_of(oz * FEAT, 8), FEAT)].astype(BF16)
        send_to(a2_send.at[oz], a2_recv.at[z], S_2DA + oz, S_2DA + z, {Z: oz})

    value = turned(z)
    for d in RING:
        oz = (z + d) % 8
        arrived(b_recv.at[oz], S_1DB + oz)
        value = value + b_recv[oz].astype(F32)
    sum_b[...] = value
    for d in RING:
        oy = (y + d) % 8
        b2_send[oy] = sum_b[pl.ds(pl.multiple_of(oy * FEAT, 8), FEAT)].astype(BF16)
        send_to(b2_send.at[oy], b2_recv.at[y], S_2DB + oy, S_2DB + y, {Y: oy})

    res_a = sum_a[pl.ds(pl.multiple_of(z * FEAT, 8), FEAT)]
    for d in RING:
        oz = (z + d) % 8
        arrived(a2_recv.at[oz], S_2DA + oz)
        res_a = res_a + a2_recv[oz].astype(F32)
    res_b = sum_b[pl.ds(pl.multiple_of(y * FEAT, 8), FEAT)]
    for d in RING:
        oy = (y + d) % 8
        arrived(b2_recv.at[oy], S_2DB + oy)
        res_b = res_b + b2_recv[oy].astype(F32)

    x_send[...] = jnp.where(xh == 0, res_b, res_a)
    send_to(x_send, x_recv, S_XH, S_XH, {XH: 1 - xh})
    arrived(x_recv, S_XH)
    o_out[...] = (jnp.where(xh == 0, res_a, res_b) + x_recv[...]).astype(BF16)

    for wait in leaving:
        wait()
    for b in range(4):
        for s in range(4):
            rows = pl.ds(*PIECES[s])

            @pl.when(q < b)
            def _():
                sent(r_send.at[b, rows], S_R + 4 * b + s)

            @pl.when(q > b)
            def _():
                sent(l_send.at[b, rows], S_L + 4 * b + s)

    for h in range(2):

        @pl.when(jnp.logical_not(mine_to[h]))
        def _():
            sent(x_in, S_X1 + h)


def hand_over(*refs):
    given, given_small, kept, kept_small, held, sems = refs[:3], refs[3], refs[4:7], refs[7], refs[8:11], refs[11]
    cuts = ((0, 112), (112, COLS - 112))
    into = [
        [pltpu.make_async_copy(a.at[pl.ds(*c)], h.at[pl.ds(*c)], sems.at[2 * i + n]) for n, c in enumerate(cuts)]
        for i, (a, h) in enumerate(zip(given, held))
    ]
    back = [
        [pltpu.make_async_copy(h.at[pl.ds(*c)], b.at[pl.ds(*c)], sems.at[6 + 2 * i + n]) for n, c in enumerate(cuts)]
        for i, (h, b) in enumerate(zip(held, kept))
    ]
    for copies in into:
        for copy in copies:
            copy.start()
    kept_small[...] = given_small[...]
    for i in range(3):
        for n in range(2):
            into[i][n].wait()
            back[i][n].start()
    for i in range(3):
        for n in range(2):
            back[i][n].wait()


def body(tok, cot, ids, adv, lens, up, first, second, rows, down):
    vmem, hbm, smem = (
        pl.BlockSpec(memory_space=pltpu.VMEM),
        pl.BlockSpec(memory_space=pl.ANY),
        pl.BlockSpec(memory_space=pltpu.SMEM),
    )

    def buf(*shape, dtype=BF16):
        return pltpu.VMEM(shape, dtype)

    out_shape = (
        jax.ShapeDtypeStruct((COLS, BLK), BF16),
        jax.ShapeDtypeStruct((COLS, BLK), F32),
        jax.ShapeDtypeStruct((COLS, BLK), F32),
        jax.ShapeDtypeStruct((FEAT, ROWS), BF16),
    )
    new_weight, new_first, new_second, out = pl.pallas_call(
        kernel,
        out_shape=out_shape,
        in_specs=[hbm, vmem, vmem, vmem, smem, hbm, hbm, hbm, vmem, hbm],
        out_specs=(hbm, hbm, hbm, vmem),
        scratch_shapes=[
            buf(4, BLK, TOK), buf(4, BLK, TOK), buf(COLS, TOK), buf(COLS, TOK),
            buf(4, COLS, BLK, dtype=F32),
            buf(4, COLS, BLK), buf(4, COLS, BLK), buf(4, COLS, BLK), buf(4, COLS, BLK),
            buf(8, 2, 8, FEAT, ROWS), buf(8, COLS, ROWS), buf(8, COLS, ROWS),
            buf(COLS, BLK), buf(COLS, BLK, dtype=F32), buf(COLS, BLK, dtype=F32),
            buf(COLS, BLK), buf(COLS, BLK, dtype=F32), buf(COLS, BLK, dtype=F32),
            buf(COLS, 8 * BLK), buf(8 * BLK, COLS), buf(8 * HALF, ROWS, dtype=F32),
            buf(8, HALF, ROWS), buf(8, HALF, ROWS), buf(8, HALF, ROWS), buf(8, HALF, ROWS),
            buf(HALF, ROWS, dtype=F32), buf(HALF, ROWS, dtype=F32), buf(HALF, ROWS, dtype=F32),
            buf(8, FEAT, ROWS), buf(8, FEAT, ROWS), buf(8, FEAT, ROWS), buf(8, FEAT, ROWS),
            buf(FEAT, ROWS, dtype=F32), buf(FEAT, ROWS, dtype=F32),
            pltpu.SemaphoreType.DMA((N_SEM,)), pltpu.SemaphoreType.DMA((N_SEM,)),
            pltpu.SemaphoreType.DMA((N_LOCAL,)),
        ],
        compiler_params=pltpu.CompilerParams(
            collective_id=0, has_side_effects=True, vmem_limit_bytes=56 * 1024 * 1024
        ),
        name="step",
    )(tok, cot.T, ids, adv, lens, up.T, first.T, second.T, rows.T, down.T)
    new_weight, new_first, new_second, out = pl.pallas_call(
        hand_over,
        out_shape=out_shape,
        in_specs=[hbm, hbm, hbm, vmem],
        out_specs=(hbm, hbm, hbm, vmem),
        scratch_shapes=[
            buf(COLS, BLK), buf(COLS, BLK, dtype=F32), buf(COLS, BLK, dtype=F32),
            pltpu.SemaphoreType.DMA((12,)),
        ],
        name="hand_over",
    )(new_weight, new_first, new_second, out)
    return (new_weight.T, new_first.T, new_second.T, out)


def solution(mesh):
    torus = Mesh(mesh.devices.reshape(4, 2, 2, 8, 8), (Q, K, XH, Y, Z))
    in_specs = (
        P(None, REP),
        P(REP, COL),
        P(REP, None),
        P(REP, None),
        P(REP, None),
        P(REP, COL),
        P(REP, COL),
        P(REP, COL),
        P(REP, COL),
        P(None, COL),
    )
    out_specs = (P(REP, COL), P(REP, COL), P(REP, COL), P(COL, REP))
    step = jax.shard_map(body, mesh=torus, in_specs=in_specs, out_specs=out_specs, check_vma=False)

    def run(tokens, cot, ids, adv, up, first, second, rows, down, lengths):
        return step(tokens, cot, ids, adv, lengths, up, first, second, rows, down)

    return run
```

```python
import math

import jax
import jax.numpy as jnp
from jax import lax
from jax.experimental import pallas as pl
from jax.experimental.pallas import tpu as pltpu
from jax.sharding import Mesh
from jax.sharding import PartitionSpec as P

SEQS = 4
REP = ("rep_0", "rep_1")
COL = ("col_0", "col_1", "col_2")
Q, K, XH, Y, Z = "rep_0", "rep_1", "col_0", "col_1", "col_2"
MESH = pl.DeviceIdType.MESH
F32 = jnp.float32
BF16 = jnp.bfloat16

first_decay = 0.9
second_decay = 0.95
learn_rate = 0.003
decay_weight = 0.1
adam_epsilon = 1e-08
first_bias = 1.0 - math.exp(100.0 * math.log(0.9))
second_bias = 1.0 - math.exp(100.0 * math.log(0.95))

BLK = 640
COLS = 216
TOK = 256
ROWS = 128
FEAT = 40
HALF = 320
PIECES = ((0, 64), (64, 64), (128, 48), (176, 40))
RING = (4, 3, 5, 2, 6, 1, 7)

S_TOK, S_SC, S_R, S_L, S_X1 = 0, 4, 5, 21, 37
S_2A, S_2B, S_3A, S_3B, S_PRE = 39, 47, 55, 63, 71
S_1DA, S_1DB, S_2DA, S_2DB, S_XH = 79, 87, 95, 103, 111
N_SEM = 112
L_TOK, L_W, L_M, L_V, L_DN, L_OUT = 0, 4, 5, 6, 7, 8
N_LOCAL = 11


def adam_update(gradient, up_weight, first_moment, second_moment):
    new_first = first_decay * first_moment + (1.0 - first_decay) * gradient
    new_second = second_decay * second_moment + (1.0 - second_decay) * gradient * gradient
    direction = new_first / first_bias / (jnp.sqrt(new_second / second_bias) + adam_epsilon)
    weight_wide = up_weight.astype(F32)
    new_weight = (weight_wide - learn_rate * (direction + decay_weight * weight_wide)).astype(BF16)
    return (new_weight, new_first, new_second)


def kernel(
    tok, cot, ids, adv, lens, w_in, m_in, v_in, x_in, down,
    w_out, m_out, v_out, o_out,
    tok_a, tok_b, sc_o, sc_p, part, r_in, l_in, r_send, l_send,
    gath, p_send, p_recv,
    w_s, m_s, v_s, w_n, m_n, v_n, dn, dn_y, dn_z,
    a_send, a_recv, b_send, b_recv, sum_a, sum_b,
    a2_send, a2_recv, b2_send, b2_recv, x_send, x_recv,
    send, recv, local,
):
    q, k = lax.axis_index(Q), lax.axis_index(K)
    xh, y, z = lax.axis_index(XH), lax.axis_index(Y), lax.axis_index(Z)
    r = 2 * q + k

    def remote(src, dst, at_send, at_recv, where):
        return pltpu.make_async_remote_copy(
            src_ref=src,
            dst_ref=dst,
            send_sem=send.at[at_send],
            recv_sem=recv.at[at_recv],
            device_id=where,
            device_id_type=MESH,
        )

    leaving = []

    def send_to(src, dst, at_send, at_recv, where):
        copy = remote(src, dst, at_send, at_recv, where)
        copy.start()
        leaving.append(copy.wait_send)

    def arrived(dst, at_recv):
        remote(dst, dst, 0, at_recv, {K: 1 - k}).wait_recv()

    def sent(src, at_send):
        remote(src, src, at_send, 0, {K: 1 - k}).wait_send()

    barrier = pltpu.get_barrier_semaphore()

    def greet(where):
        pl.semaphore_signal(barrier, inc=1, device_id=where, device_id_type=MESH)

    from_q, from_k, from_x = y // 2, y % 2, q // 2
    from_y = [4 * (q % 2) + 2 * k + j for j in range(2)]
    mine_from = [(from_q == q) & (from_k == k) & (from_x == xh) & (from_y[j] == y) for j in range(2)]
    to_q, to_k = 2 * xh + y // 4, (y // 2) % 2
    mine_to = [(to_q == q) & (to_k == k) & (xh == h) & (r == y) for h in range(2)]

    for d in range(1, 8):
        other = (r + d) % 8
        greet({Q: other // 2, K: other % 2})
        greet({Y: (y + d) % 8})
        greet({Z: (z + d) % 8})
    greet({XH: 1 - xh})
    for j in range(2):

        @pl.when(jnp.logical_not(mine_from[j]))
        def _():
            greet({Q: from_q, K: from_k, XH: from_x, Y: from_y[j], Z: z})

    def block_rows(b, parity):
        return pl.ds(pl.multiple_of((2 * b + parity) * BLK, BLK), BLK)

    order = (3, 0, 2, 1)
    loads = [pltpu.make_async_copy(tok.at[block_rows(b, k)], tok_a.at[b], local.at[L_TOK + b]) for b in range(4)]
    for b in order:
        loads[b].start()
    late = [
        pltpu.make_async_copy(w_in, w_s, local.at[L_W]),
        pltpu.make_async_copy(m_in, m_s, local.at[L_M]),
        pltpu.make_async_copy(v_in, v_s, local.at[L_V]),
        pltpu.make_async_copy(down, dn, local.at[L_DN]),
    ]
    for copy in late:
        copy.start()

    sample = lax.broadcasted_iota(jnp.int32, (8, TOK), 0)
    members = (ids[...] == sample).astype(F32)
    counts = jnp.sum(members, axis=1, keepdims=True)
    eye = lax.broadcasted_iota(jnp.int32, (8, 8), 0) == lax.broadcasted_iota(jnp.int32, (8, 8), 1)
    tall = jnp.sum(jnp.where(eye, adv[...], 0.0), axis=1, keepdims=True)
    scale = jnp.sum(members * (tall / counts), axis=0, keepdims=True)
    sc_o[...] = (scale * cot[...].astype(F32)).astype(BF16)

    pl.semaphore_wait(barrier, 24 - mine_to[0].astype(jnp.int32) - mine_to[1].astype(jnp.int32))

    for h in range(2):

        @pl.when(jnp.logical_not(mine_to[h]))
        def _():
            remote(x_in, gath.at[r, y % 2, z], S_X1 + h, S_X1 + y % 2, {Q: to_q, K: to_k, XH: h, Y: r, Z: z}).start()

        @pl.when(mine_to[h])
        def _():
            gath[r, y % 2, z] = x_in[...]

    send_to(sc_o, sc_p, S_SC, S_SC, {K: 1 - k})
    for b in order:
        send_to(tok.at[block_rows(b, 1 - k)], tok_b.at[b], S_TOK + b, S_TOK + b, {K: 1 - k})

    def running(b, s, first, sums, out, at, target):
        rows = pl.ds(*PIECES[s])
        value = part[b, rows]
        if not first:
            arrived(sums.at[b, rows], at + 4 * b + s)
            value = value + sums[b, rows].astype(F32)
        out[b, rows] = value.astype(BF16)
        remote(out.at[b, rows], sums.at[b, rows], at + 4 * b + s, at + 4 * b + s, {Q: target}).start()

    def right(b, s, first):
        running(b, s, first, r_in, r_send, S_R, q + 1)

    def left(b, s, first):
        running(b, s, first, l_in, l_send, S_L, q - 1)

    def over_tokens(scaled, tokens):
        return lax.dot_general(scaled, tokens, (((1,), (1,)), ((), ())), preferred_element_type=F32)

    arrived(sc_p, S_SC)
    for b in order:
        loads[b].wait()
        arrived(tok_b.at[b], S_TOK + b)

        part[b] = over_tokens(sc_o[...], tok_a[b]) + over_tokens(sc_p[...], tok_b[b])

        if b > 0:

            @pl.when(q == 0)
            def _():
                for s in range(4):
                    right(b, s, True)

        if b < 3:

            @pl.when(q == 3)
            def _():
                for s in range(4):
                    left(b, s, True)

    for j in range(2):

        @pl.when(jnp.logical_not(mine_from[j]))
        def _():
            arrived(gath.at[y, j, z], S_X1 + j)

    for d in RING:
        oz, oy = (z + d) % 8, (y + d) % 8
        here = gath.at[y, 0, z]
        send_to(here, here, S_2A + oz, S_2A + z, {Z: oz})
        here = gath.at[y, 1, z]
        send_to(here, here, S_2B + oy, S_2B + y, {Y: oy})

    @pl.when(q == 1)
    def _():
        for s in range(4):
            right(3, s, False)

    @pl.when(q == 2)
    def _():
        for s in range(4):
            left(0, s, False)

    for d in reversed(RING):
        oz = (z + d) % 8
        arrived(gath.at[y, 0, oz], S_2A + oz)
    for d in RING:
        oy = (y + d) % 8
        here = gath.at[y, 0]
        send_to(here, here, S_3A + oy, S_3A + y, {Y: oy})
    for d in reversed(RING):
        oy = (y + d) % 8
        arrived(gath.at[oy, 1, z], S_2B + oy)
    for d in RING:
        oz = (z + d) % 8
        here = gath.at[:, 1, z]
        send_to(here, here, S_3B + oz, S_3B + z, {Z: oz})

    @pl.when(q == 1)
    def _():
        for s in range(4):
            left(0, s, False)
        for s in range(4):
            right(2, s, False)

    @pl.when(q == 2)
    def _():
        for s in range(4):
            right(3, s, False)
        for s in range(4):
            left(1, s, False)

    late[3].wait()

    def turned(at):
        wide = jnp.concatenate([dn[:, at].astype(F32), jnp.zeros((256 - COLS, BLK), F32)], axis=0)
        return jnp.transpose(wide)[:, :COLS]

    @pl.loop(0, 4)
    def _(i):
        near = turned(pl.ds(pl.multiple_of(i * BLK, BLK), BLK)).astype(BF16)
        dn_y[2 * i] = near[:HALF]
        dn_y[2 * i + 1] = near[HALF:]
        far = turned(pl.ds(pl.multiple_of((4 + i) * BLK, BLK), BLK))
        for j in range(2):
            for n in range(8):
                at = j * HALF + n * FEAT
                dn_z[n, 2 * i + j] = far[at : at + FEAT].astype(BF16)

    @pl.when(q > 0)
    def _():
        for s in range(4):
            arrived(r_in.at[q, pl.ds(*PIECES[s])], S_R + 4 * q + s)

    @pl.when(q < 3)
    def _():
        for s in range(4):
            arrived(l_in.at[q, pl.ds(*PIECES[s])], S_L + 4 * q + s)

    for copy in late[:3]:
        copy.wait()
    has_left, has_right = q > 0, q < 3

    @pl.loop(0, 5)
    def _(i):
        lanes = pl.ds(pl.multiple_of(i * 128, 128), 128)
        for piece in PIECES:
            rows = pl.ds(*piece)
            gradient = part[q, rows, lanes]
            gradient = gradient + jnp.where(has_left, r_in[q, rows, lanes].astype(F32), 0.0)
            gradient = gradient + jnp.where(has_right, l_in[q, rows, lanes].astype(F32), 0.0)
            new = adam_update(gradient, w_s[rows, lanes], m_s[rows, lanes], v_s[rows, lanes])
            w_n[rows, lanes], m_n[rows, lanes], v_n[rows, lanes] = new

    outs = [
        pltpu.make_async_copy(w_n, w_out, local.at[L_OUT]),
        pltpu.make_async_copy(m_n, m_out, local.at[L_OUT + 1]),
        pltpu.make_async_copy(v_n, v_out, local.at[L_OUT + 2]),
    ]
    for copy in outs:
        copy.start()
        leaving.append(copy.wait)

    for d in RING:
        oy, oz = (y + d) % 8, (z + d) % 8
        arrived(gath.at[oy, 0], S_3A + oy)
        arrived(gath.at[:, 1, oz], S_3B + oz)

    def partial_of(other):
        return jnp.dot(w_n[...], gath[other].reshape(BLK, ROWS), preferred_element_type=F32)

    for d in (7, 6, 5, 4, 3, 2, 1):
        other = (r + d) % 8
        p_send[other] = partial_of(other).astype(BF16)
        send_to(p_send.at[other], p_recv.at[r], S_PRE + other, S_PRE + r, {Q: other // 2, K: other % 2})
    pre = partial_of(r)
    for d in range(1, 8):
        other = (r + d) % 8
        arrived(p_recv.at[other], S_PRE + other)
        pre = pre + p_recv[other].astype(F32)

    lane = lax.broadcasted_iota(jnp.int32, (1, ROWS), 1)
    slot_len = ROWS // SEQS
    limit = jnp.zeros((1, ROWS), jnp.int32)
    for s in range(SEQS):
        limit = jnp.where(lane // slot_len == s, lens[0, s], limit)
    live = lane % slot_len < limit
    act = jnp.where(live, pre / (1.0 + jnp.exp(-pre)), 0.0).astype(BF16)

    def down_y(oy):
        return jnp.dot(dn_y[oy], act, preferred_element_type=F32)

    def down_z(oz):
        return jnp.dot(dn_z[oz].reshape(HALF, COLS), act, preferred_element_type=F32)

    for d in RING:
        oy, oz = (y + d) % 8, (z + d) % 8
        a_send[oy] = down_y(oy).astype(BF16)
        send_to(a_send.at[oy], a_recv.at[y], S_1DA + oy, S_1DA + y, {Y: oy})
        b_send[oz] = down_z(oz).astype(BF16)
        send_to(b_send.at[oz], b_recv.at[z], S_1DB + oz, S_1DB + z, {Z: oz})
    sum_a[...] = down_y(y)
    sum_b[...] = down_z(z)

    value = sum_a[...]
    for d in RING:
        oy = (y + d) % 8
        arrived(a_recv.at[oy], S_1DA + oy)
        value = value + a_recv[oy].astype(F32)
    sum_a[...] = value
    for d in RING:
        oz = (z + d) % 8
        a2_send[oz] = sum_a[pl.ds(pl.multiple_of(oz * FEAT, 8), FEAT)].astype(BF16)
        send_to(a2_send.at[oz], a2_recv.at[z], S_2DA + oz, S_2DA + z, {Z: oz})

    value = sum_b[...]
    for d in RING:
        oz = (z + d) % 8
        arrived(b_recv.at[oz], S_1DB + oz)
        value = value + b_recv[oz].astype(F32)
    sum_b[...] = value
    for d in RING:
        oy = (y + d) % 8
        b2_send[oy] = sum_b[pl.ds(pl.multiple_of(oy * FEAT, 8), FEAT)].astype(BF16)
        send_to(b2_send.at[oy], b2_recv.at[y], S_2DB + oy, S_2DB + y, {Y: oy})

    res_a = sum_a[pl.ds(pl.multiple_of(z * FEAT, 8), FEAT)]
    for d in RING:
        oz = (z + d) % 8
        arrived(a2_recv.at[oz], S_2DA + oz)
        res_a = res_a + a2_recv[oz].astype(F32)
    res_b = sum_b[pl.ds(pl.multiple_of(y * FEAT, 8), FEAT)]
    for d in RING:
        oy = (y + d) % 8
        arrived(b2_recv.at[oy], S_2DB + oy)
        res_b = res_b + b2_recv[oy].astype(F32)

    x_send[...] = jnp.where(xh == 0, res_b, res_a)
    send_to(x_send, x_recv, S_XH, S_XH, {XH: 1 - xh})
    arrived(x_recv, S_XH)
    o_out[...] = (jnp.where(xh == 0, res_a, res_b) + x_recv[...]).astype(BF16)

    for wait in leaving:
        wait()
    for b in range(4):
        for s in range(4):
            rows = pl.ds(*PIECES[s])

            @pl.when(q < b)
            def _():
                sent(r_send.at[b, rows], S_R + 4 * b + s)

            @pl.when(q > b)
            def _():
                sent(l_send.at[b, rows], S_L + 4 * b + s)

    for h in range(2):

        @pl.when(jnp.logical_not(mine_to[h]))
        def _():
            sent(x_in, S_X1 + h)


def hand_over(*refs):
    given, given_small, kept, kept_small, held, sems = refs[:3], refs[3], refs[4:7], refs[7], refs[8:11], refs[11]
    cuts = ((0, 112), (112, COLS - 112))
    into = [
        [pltpu.make_async_copy(a.at[pl.ds(*c)], h.at[pl.ds(*c)], sems.at[2 * i + n]) for n, c in enumerate(cuts)]
        for i, (a, h) in enumerate(zip(given, held))
    ]
    back = [
        [pltpu.make_async_copy(h.at[pl.ds(*c)], b.at[pl.ds(*c)], sems.at[6 + 2 * i + n]) for n, c in enumerate(cuts)]
        for i, (h, b) in enumerate(zip(held, kept))
    ]
    for copies in into:
        for copy in copies:
            copy.start()
    kept_small[...] = given_small[...]
    for i in range(3):
        for n in range(2):
            into[i][n].wait()
            back[i][n].start()
    for i in range(3):
        for n in range(2):
            back[i][n].wait()


def body(tok, cot, ids, adv, lens, up, first, second, rows, down):
    vmem, hbm, smem = (
        pl.BlockSpec(memory_space=pltpu.VMEM),
        pl.BlockSpec(memory_space=pl.ANY),
        pl.BlockSpec(memory_space=pltpu.SMEM),
    )

    def buf(*shape, dtype=BF16):
        return pltpu.VMEM(shape, dtype)

    out_shape = (
        jax.ShapeDtypeStruct((COLS, BLK), BF16),
        jax.ShapeDtypeStruct((COLS, BLK), F32),
        jax.ShapeDtypeStruct((COLS, BLK), F32),
        jax.ShapeDtypeStruct((FEAT, ROWS), BF16),
    )
    new_weight, new_first, new_second, out = pl.pallas_call(
        kernel,
        out_shape=out_shape,
        in_specs=[hbm, vmem, vmem, vmem, smem, hbm, hbm, hbm, vmem, hbm],
        out_specs=(hbm, hbm, hbm, vmem),
        scratch_shapes=[
            buf(4, BLK, TOK), buf(4, BLK, TOK), buf(COLS, TOK), buf(COLS, TOK),
            buf(4, COLS, BLK, dtype=F32),
            buf(4, COLS, BLK), buf(4, COLS, BLK), buf(4, COLS, BLK), buf(4, COLS, BLK),
            buf(8, 2, 8, FEAT, ROWS), buf(8, COLS, ROWS), buf(8, COLS, ROWS),
            buf(COLS, BLK), buf(COLS, BLK, dtype=F32), buf(COLS, BLK, dtype=F32),
            buf(COLS, BLK), buf(COLS, BLK, dtype=F32), buf(COLS, BLK, dtype=F32),
            buf(COLS, 8 * BLK), buf(8, HALF, COLS), buf(8, 8, FEAT, COLS),
            buf(8, HALF, ROWS), buf(8, HALF, ROWS), buf(8, HALF, ROWS), buf(8, HALF, ROWS),
            buf(HALF, ROWS, dtype=F32), buf(HALF, ROWS, dtype=F32),
            buf(8, FEAT, ROWS), buf(8, FEAT, ROWS), buf(8, FEAT, ROWS), buf(8, FEAT, ROWS),
            buf(FEAT, ROWS, dtype=F32), buf(FEAT, ROWS, dtype=F32),
            pltpu.SemaphoreType.DMA((N_SEM,)), pltpu.SemaphoreType.DMA((N_SEM,)),
            pltpu.SemaphoreType.DMA((N_LOCAL,)),
        ],
        compiler_params=pltpu.CompilerParams(
            collective_id=0, has_side_effects=True, vmem_limit_bytes=56 * 1024 * 1024
        ),
        name="step",
    )(tok, cot.T, ids, adv, lens, up.T, first.T, second.T, rows.T, down.T)
    new_weight, new_first, new_second, out = pl.pallas_call(
        hand_over,
        out_shape=out_shape,
        in_specs=[hbm, hbm, hbm, vmem],
        out_specs=(hbm, hbm, hbm, vmem),
        scratch_shapes=[
            buf(COLS, BLK), buf(COLS, BLK, dtype=F32), buf(COLS, BLK, dtype=F32),
            pltpu.SemaphoreType.DMA((12,)),
        ],
        name="hand_over",
    )(new_weight, new_first, new_second, out)
    return (new_weight.T, new_first.T, new_second.T, out)


def solution(mesh):
    torus = Mesh(mesh.devices.reshape(4, 2, 2, 8, 8), (Q, K, XH, Y, Z))
    in_specs = (
        P(None, REP),
        P(REP, COL),
        P(REP, None),
        P(REP, None),
        P(REP, None),
        P(REP, COL),
        P(REP, COL),
        P(REP, COL),
        P(REP, COL),
        P(None, COL),
    )
    out_specs = (P(REP, COL), P(REP, COL), P(REP, COL), P(COL, REP))
    step = jax.shard_map(body, mesh=torus, in_specs=in_specs, out_specs=out_specs, check_vma=False)

    def run(tokens, cot, ids, adv, up, first, second, rows, down, lengths):
        return step(tokens, cot, ids, adv, lengths, up, first, second, rows, down)

    return run
```

```python
import math

import jax
import jax.numpy as jnp
from jax import lax
from jax.experimental import pallas as pl
from jax.experimental.pallas import tpu as pltpu
from jax.sharding import Mesh
from jax.sharding import PartitionSpec as P

SEQS = 4
REP = ("rep_0", "rep_1")
COL = ("col_0", "col_1", "col_2")
Q, K, XH, Y, Z = "rep_0", "rep_1", "col_0", "col_1", "col_2"
MESH = pl.DeviceIdType.MESH
F32 = jnp.float32
BF16 = jnp.bfloat16

first_decay = 0.9
second_decay = 0.95
learn_rate = 0.003
decay_weight = 0.1
adam_epsilon = 1e-08
first_bias = 1.0 - math.exp(100.0 * math.log(0.9))
second_bias = 1.0 - math.exp(100.0 * math.log(0.95))

BLK = 640
COLS = 216
TOK = 256
ROWS = 128
FEAT = 40
HALF = 320
LIVE = 96
FOLD_COLS = 168
FOLD_HALF = 240
PIECES = ((0, 64), (64, 64), (128, 48), (176, 40))
RING = (4, 3, 5, 2, 6, 1, 7)

S_TOK, S_SC, S_R, S_L, S_X1 = 0, 4, 5, 21, 37
S_2A, S_2B, S_3A, S_3B, S_PRE = 39, 47, 55, 63, 71
S_1DA, S_1DB, S_2DA, S_2DB, S_XH = 79, 87, 95, 103, 111
N_SEM = 112
L_TOK, L_W, L_M, L_V, L_DN, L_OUT = 0, 4, 5, 6, 7, 8
N_LOCAL = 11


def adam_update(gradient, up_weight, first_moment, second_moment):
    new_first = first_decay * first_moment + (1.0 - first_decay) * gradient
    new_second = second_decay * second_moment + (1.0 - second_decay) * gradient * gradient
    direction = new_first / first_bias / (jnp.sqrt(new_second / second_bias) + adam_epsilon)
    weight_wide = up_weight.astype(F32)
    new_weight = (weight_wide - learn_rate * (direction + decay_weight * weight_wide)).astype(BF16)
    return (new_weight, new_first, new_second)


def fold(value, rows):
    quarter = value.shape[0] - rows
    tail = value[rows:]
    side = [pltpu.roll(tail, LIVE - 32 * s, 1) for s in range(3)]
    if 3 * quarter < rows:
        side.append(jnp.zeros((rows - 3 * quarter, ROWS), F32))
    lane = lax.broadcasted_iota(jnp.int32, (rows, ROWS), 1)
    return jnp.where(lane < LIVE, value[:rows], jnp.concatenate(side, axis=0))


def unfold(value, length):
    rows = value.shape[0]
    quarter = length - rows
    side = [pltpu.roll(value[s * quarter : (s + 1) * quarter], 32 + 32 * s, 1) for s in range(3)]
    lane = lax.broadcasted_iota(jnp.int32, (quarter, ROWS), 1)
    tail = jnp.where(lane < 32, side[0], jnp.where(lane < 64, side[1], side[2]))
    whole = jnp.concatenate([value, tail], axis=0)
    return jnp.where(lax.broadcasted_iota(jnp.int32, (length, ROWS), 1) < LIVE, whole, 0.0)


def picks(lens, dim):
    row = lax.broadcasted_iota(jnp.int32, (ROWS, ROWS), dim)
    place = lax.broadcasted_iota(jnp.int32, (ROWS, ROWS), 1 - dim)
    slot_len = ROWS // SEQS
    slot, within = row // slot_len, row % slot_len
    limit, ahead = jnp.zeros_like(row), jnp.zeros_like(row)
    before = jnp.int32(0)
    for s in range(SEQS):
        limit = jnp.where(slot == s, lens[0, s], limit)
        ahead = jnp.where(slot == s, before, ahead)
        before = before + lens[0, s]
    return jnp.where((within < limit) & (ahead + within == place), 1.0, 0.0).astype(BF16)


def kernel(
    tok, cot, ids, adv, lens, w_in, m_in, v_in, x_in, down,
    w_out, m_out, v_out, o_out,
    tok_a, tok_b, sc_o, sc_p, part, r_in, l_in, r_send, l_send,
    x_live, gath, p_send, p_recv,
    w_s, m_s, v_s, w_n, m_n, v_n, dn, dn_y, dn_z,
    a_send, a_recv, b_send, b_recv, sum_a, sum_b,
    a2_send, a2_recv, b2_send, b2_recv, x_send, x_recv,
    send, recv, local,
):
    q, k = lax.axis_index(Q), lax.axis_index(K)
    xh, y, z = lax.axis_index(XH), lax.axis_index(Y), lax.axis_index(Z)
    r = 2 * q + k

    def remote(src, dst, at_send, at_recv, where):
        return pltpu.make_async_remote_copy(
            src_ref=src,
            dst_ref=dst,
            send_sem=send.at[at_send],
            recv_sem=recv.at[at_recv],
            device_id=where,
            device_id_type=MESH,
        )

    leaving = []

    def send_to(src, dst, at_send, at_recv, where):
        copy = remote(src, dst, at_send, at_recv, where)
        copy.start()
        leaving.append(copy.wait_send)

    def arrived(dst, at_recv):
        remote(dst, dst, 0, at_recv, {K: 1 - k}).wait_recv()

    def sent(src, at_send):
        remote(src, src, at_send, 0, {K: 1 - k}).wait_send()

    barrier = pltpu.get_barrier_semaphore()

    def greet(where):
        pl.semaphore_signal(barrier, inc=1, device_id=where, device_id_type=MESH)

    from_q, from_k, from_x = y // 2, y % 2, q // 2
    from_y = [4 * (q % 2) + 2 * k + j for j in range(2)]
    mine_from = [(from_q == q) & (from_k == k) & (from_x == xh) & (from_y[j] == y) for j in range(2)]
    to_q, to_k = 2 * xh + y // 4, (y // 2) % 2
    mine_to = [(to_q == q) & (to_k == k) & (xh == h) & (r == y) for h in range(2)]

    for d in range(1, 8):
        other = (r + d) % 8
        greet({Q: other // 2, K: other % 2})
        greet({Y: (y + d) % 8})
        greet({Z: (z + d) % 8})
    greet({XH: 1 - xh})
    for j in range(2):

        @pl.when(jnp.logical_not(mine_from[j]))
        def _():
            greet({Q: from_q, K: from_k, XH: from_x, Y: from_y[j], Z: z})

    def block_rows(b, parity):
        return pl.ds(pl.multiple_of((2 * b + parity) * BLK, BLK), BLK)

    order = (3, 0, 2, 1)
    loads = [pltpu.make_async_copy(tok.at[block_rows(b, k)], tok_a.at[b], local.at[L_TOK + b]) for b in range(4)]
    for b in order:
        loads[b].start()
    late = [
        pltpu.make_async_copy(w_in, w_s, local.at[L_W]),
        pltpu.make_async_copy(m_in, m_s, local.at[L_M]),
        pltpu.make_async_copy(v_in, v_s, local.at[L_V]),
        pltpu.make_async_copy(down, dn, local.at[L_DN]),
    ]
    for copy in late:
        copy.start()

    x_live[...] = jnp.dot(x_in[...], picks(lens, 0), preferred_element_type=F32).astype(BF16)

    sample = lax.broadcasted_iota(jnp.int32, (8, TOK), 0)
    members = (ids[...] == sample).astype(F32)
    counts = jnp.sum(members, axis=1, keepdims=True)
    eye = lax.broadcasted_iota(jnp.int32, (8, 8), 0) == lax.broadcasted_iota(jnp.int32, (8, 8), 1)
    tall = jnp.sum(jnp.where(eye, adv[...], 0.0), axis=1, keepdims=True)
    scale = jnp.sum(members * (tall / counts), axis=0, keepdims=True)
    sc_o[...] = (scale * cot[...].astype(F32)).astype(BF16)

    pl.semaphore_wait(barrier, 24 - mine_to[0].astype(jnp.int32) - mine_to[1].astype(jnp.int32))

    for h in range(2):

        @pl.when(jnp.logical_not(mine_to[h]))
        def _():
            remote(x_live, gath.at[r, y % 2, z], S_X1 + h, S_X1 + y % 2, {Q: to_q, K: to_k, XH: h, Y: r, Z: z}).start()

        @pl.when(mine_to[h])
        def _():
            gath[r, y % 2, z] = x_live[...]

    send_to(sc_o, sc_p, S_SC, S_SC, {K: 1 - k})
    for b in order:
        send_to(tok.at[block_rows(b, 1 - k)], tok_b.at[b], S_TOK + b, S_TOK + b, {K: 1 - k})

    def running(b, s, first, sums, out, at, target):
        rows = pl.ds(*PIECES[s])
        value = part[b, rows]
        if not first:
            arrived(sums.at[b, rows], at + 4 * b + s)
            value = value + sums[b, rows].astype(F32)
        out[b, rows] = value.astype(BF16)
        remote(out.at[b, rows], sums.at[b, rows], at + 4 * b + s, at + 4 * b + s, {Q: target}).start()

    def right(b, s, first):
        running(b, s, first, r_in, r_send, S_R, q + 1)

    def left(b, s, first):
        running(b, s, first, l_in, l_send, S_L, q - 1)

    def over_tokens(scaled, tokens):
        return lax.dot_general(scaled, tokens, (((1,), (1,)), ((), ())), preferred_element_type=F32)

    arrived(sc_p, S_SC)
    for b in order:
        loads[b].wait()
        arrived(tok_b.at[b], S_TOK + b)

        part[b] = over_tokens(sc_o[...], tok_a[b]) + over_tokens(sc_p[...], tok_b[b])

        if b > 0:

            @pl.when(q == 0)
            def _():
                for s in range(4):
                    right(b, s, True)

        if b < 3:

            @pl.when(q == 3)
            def _():
                for s in range(4):
                    left(b, s, True)

    for j in range(2):

        @pl.when(jnp.logical_not(mine_from[j]))
        def _():
            arrived(gath.at[y, j, z], S_X1 + j)

    for d in RING:
        oz, oy = (z + d) % 8, (y + d) % 8
        here = gath.at[y, 0, z]
        send_to(here, here, S_2A + oz, S_2A + z, {Z: oz})
        here = gath.at[y, 1, z]
        send_to(here, here, S_2B + oy, S_2B + y, {Y: oy})

    @pl.when(q == 1)
    def _():
        for s in range(4):
            right(3, s, False)

    @pl.when(q == 2)
    def _():
        for s in range(4):
            left(0, s, False)

    for d in reversed(RING):
        oz = (z + d) % 8
        arrived(gath.at[y, 0, oz], S_2A + oz)
    for d in RING:
        oy = (y + d) % 8
        here = gath.at[y, 0]
        send_to(here, here, S_3A + oy, S_3A + y, {Y: oy})
    for d in reversed(RING):
        oy = (y + d) % 8
        arrived(gath.at[oy, 1, z], S_2B + oy)
    for d in RING:
        oz = (z + d) % 8
        here = gath.at[:, 1, z]
        send_to(here, here, S_3B + oz, S_3B + z, {Z: oz})

    @pl.when(q == 1)
    def _():
        for s in range(4):
            left(0, s, False)
        for s in range(4):
            right(2, s, False)

    @pl.when(q == 2)
    def _():
        for s in range(4):
            right(3, s, False)
        for s in range(4):
            left(1, s, False)

    late[3].wait()

    def turned(at):
        wide = jnp.concatenate([dn[:, at].astype(F32), jnp.zeros((256 - COLS, BLK), F32)], axis=0)
        return jnp.transpose(wide)[:, :COLS]

    @pl.loop(0, 4)
    def _(i):
        near = turned(pl.ds(pl.multiple_of(i * BLK, BLK), BLK)).astype(BF16)
        dn_y[2 * i] = near[:HALF]
        dn_y[2 * i + 1] = near[HALF:]
        far = turned(pl.ds(pl.multiple_of((4 + i) * BLK, BLK), BLK))
        for j in range(2):
            for n in range(8):
                at = j * HALF + n * FEAT
                dn_z[n, 2 * i + j] = far[at : at + FEAT].astype(BF16)

    @pl.when(q > 0)
    def _():
        for s in range(4):
            arrived(r_in.at[q, pl.ds(*PIECES[s])], S_R + 4 * q + s)

    @pl.when(q < 3)
    def _():
        for s in range(4):
            arrived(l_in.at[q, pl.ds(*PIECES[s])], S_L + 4 * q + s)

    for copy in late[:3]:
        copy.wait()
    has_left, has_right = q > 0, q < 3

    @pl.loop(0, 5)
    def _(i):
        lanes = pl.ds(pl.multiple_of(i * 128, 128), 128)
        for piece in PIECES:
            rows = pl.ds(*piece)
            gradient = part[q, rows, lanes]
            gradient = gradient + jnp.where(has_left, r_in[q, rows, lanes].astype(F32), 0.0)
            gradient = gradient + jnp.where(has_right, l_in[q, rows, lanes].astype(F32), 0.0)
            new = adam_update(gradient, w_s[rows, lanes], m_s[rows, lanes], v_s[rows, lanes])
            w_n[rows, lanes], m_n[rows, lanes], v_n[rows, lanes] = new

    outs = [
        pltpu.make_async_copy(w_n, w_out, local.at[L_OUT]),
        pltpu.make_async_copy(m_n, m_out, local.at[L_OUT + 1]),
        pltpu.make_async_copy(v_n, v_out, local.at[L_OUT + 2]),
    ]
    for copy in outs:
        copy.start()
        leaving.append(copy.wait)

    for d in RING:
        oy, oz = (y + d) % 8, (z + d) % 8
        arrived(gath.at[oy, 0], S_3A + oy)
        arrived(gath.at[:, 1, oz], S_3B + oz)

    def partial_of(other):
        return fold(jnp.dot(w_n[...], gath[other].reshape(BLK, ROWS), preferred_element_type=F32), FOLD_COLS)

    for d in (7, 6, 5, 4, 3, 2, 1):
        other = (r + d) % 8
        p_send[other] = partial_of(other).astype(BF16)
        send_to(p_send.at[other], p_recv.at[r], S_PRE + other, S_PRE + r, {Q: other // 2, K: other % 2})
    pre = partial_of(r)
    for d in range(1, 8):
        other = (r + d) % 8
        arrived(p_recv.at[other], S_PRE + other)
        pre = pre + p_recv[other].astype(F32)

    pre = unfold(pre, COLS)
    act = (pre / (1.0 + jnp.exp(-pre))).astype(BF16)

    def down_y(oy):
        return fold(jnp.dot(dn_y[oy], act, preferred_element_type=F32), FOLD_HALF)

    def down_z(oz):
        return fold(jnp.dot(dn_z[oz].reshape(HALF, COLS), act, preferred_element_type=F32), FOLD_HALF)

    for d in RING:
        oy, oz = (y + d) % 8, (z + d) % 8
        a_send[oy] = down_y(oy).astype(BF16)
        send_to(a_send.at[oy], a_recv.at[y], S_1DA + oy, S_1DA + y, {Y: oy})
        b_send[oz] = down_z(oz).astype(BF16)
        send_to(b_send.at[oz], b_recv.at[z], S_1DB + oz, S_1DB + z, {Z: oz})
    own_a, own_b = down_y(y), down_z(z)

    value = own_a
    for d in RING:
        oy = (y + d) % 8
        arrived(a_recv.at[oy], S_1DA + oy)
        value = value + a_recv[oy].astype(F32)
    sum_a[...] = unfold(value, HALF)
    for d in RING:
        oz = (z + d) % 8
        a2_send[oz] = sum_a[pl.ds(pl.multiple_of(oz * FEAT, 8), FEAT)].astype(BF16)
        send_to(a2_send.at[oz], a2_recv.at[z], S_2DA + oz, S_2DA + z, {Z: oz})

    value = own_b
    for d in RING:
        oz = (z + d) % 8
        arrived(b_recv.at[oz], S_1DB + oz)
        value = value + b_recv[oz].astype(F32)
    sum_b[...] = unfold(value, HALF)
    for d in RING:
        oy = (y + d) % 8
        b2_send[oy] = sum_b[pl.ds(pl.multiple_of(oy * FEAT, 8), FEAT)].astype(BF16)
        send_to(b2_send.at[oy], b2_recv.at[y], S_2DB + oy, S_2DB + y, {Y: oy})

    res_a = sum_a[pl.ds(pl.multiple_of(z * FEAT, 8), FEAT)]
    for d in RING:
        oz = (z + d) % 8
        arrived(a2_recv.at[oz], S_2DA + oz)
        res_a = res_a + a2_recv[oz].astype(F32)
    res_b = sum_b[pl.ds(pl.multiple_of(y * FEAT, 8), FEAT)]
    for d in RING:
        oy = (y + d) % 8
        arrived(b2_recv.at[oy], S_2DB + oy)
        res_b = res_b + b2_recv[oy].astype(F32)

    x_send[...] = jnp.where(xh == 0, res_b, res_a)
    send_to(x_send, x_recv, S_XH, S_XH, {XH: 1 - xh})
    arrived(x_recv, S_XH)
    total = (jnp.where(xh == 0, res_a, res_b) + x_recv[...]).astype(BF16)
    o_out[...] = jnp.dot(total, picks(lens, 1), preferred_element_type=F32).astype(BF16)

    for wait in leaving:
        wait()
    for b in range(4):
        for s in range(4):
            rows = pl.ds(*PIECES[s])

            @pl.when(q < b)
            def _():
                sent(r_send.at[b, rows], S_R + 4 * b + s)

            @pl.when(q > b)
            def _():
                sent(l_send.at[b, rows], S_L + 4 * b + s)

    for h in range(2):

        @pl.when(jnp.logical_not(mine_to[h]))
        def _():
            sent(x_live, S_X1 + h)


def hand_over(*refs):
    given, given_small, kept, kept_small, held, sems = refs[:3], refs[3], refs[4:7], refs[7], refs[8:11], refs[11]
    cuts = ((0, 112), (112, COLS - 112))
    into = [
        [pltpu.make_async_copy(a.at[pl.ds(*c)], h.at[pl.ds(*c)], sems.at[2 * i + n]) for n, c in enumerate(cuts)]
        for i, (a, h) in enumerate(zip(given, held))
    ]
    back = [
        [pltpu.make_async_copy(h.at[pl.ds(*c)], b.at[pl.ds(*c)], sems.at[6 + 2 * i + n]) for n, c in enumerate(cuts)]
        for i, (h, b) in enumerate(zip(held, kept))
    ]
    for copies in into:
        for copy in copies:
            copy.start()
    kept_small[...] = given_small[...]
    for i in range(3):
        for n in range(2):
            into[i][n].wait()
            back[i][n].start()
    for i in range(3):
        for n in range(2):
            back[i][n].wait()


def body(tok, cot, ids, adv, lens, up, first, second, rows, down):
    vmem, hbm, smem = (
        pl.BlockSpec(memory_space=pltpu.VMEM),
        pl.BlockSpec(memory_space=pl.ANY),
        pl.BlockSpec(memory_space=pltpu.SMEM),
    )

    def buf(*shape, dtype=BF16):
        return pltpu.VMEM(shape, dtype)

    out_shape = (
        jax.ShapeDtypeStruct((COLS, BLK), BF16),
        jax.ShapeDtypeStruct((COLS, BLK), F32),
        jax.ShapeDtypeStruct((COLS, BLK), F32),
        jax.ShapeDtypeStruct((FEAT, ROWS), BF16),
    )
    new_weight, new_first, new_second, out = pl.pallas_call(
        kernel,
        out_shape=out_shape,
        in_specs=[hbm, vmem, vmem, vmem, smem, hbm, hbm, hbm, vmem, hbm],
        out_specs=(hbm, hbm, hbm, vmem),
        scratch_shapes=[
            buf(4, BLK, TOK), buf(4, BLK, TOK), buf(COLS, TOK), buf(COLS, TOK),
            buf(4, COLS, BLK, dtype=F32),
            buf(4, COLS, BLK), buf(4, COLS, BLK), buf(4, COLS, BLK), buf(4, COLS, BLK),
            buf(FEAT, ROWS), buf(8, 2, 8, FEAT, ROWS), buf(8, FOLD_COLS, ROWS), buf(8, FOLD_COLS, ROWS),
            buf(COLS, BLK), buf(COLS, BLK, dtype=F32), buf(COLS, BLK, dtype=F32),
            buf(COLS, BLK), buf(COLS, BLK, dtype=F32), buf(COLS, BLK, dtype=F32),
            buf(COLS, 8 * BLK), buf(8, HALF, COLS), buf(8, 8, FEAT, COLS),
            buf(8, FOLD_HALF, ROWS), buf(8, FOLD_HALF, ROWS), buf(8, FOLD_HALF, ROWS), buf(8, FOLD_HALF, ROWS),
            buf(HALF, ROWS, dtype=F32), buf(HALF, ROWS, dtype=F32),
            buf(8, FEAT, ROWS), buf(8, FEAT, ROWS), buf(8, FEAT, ROWS), buf(8, FEAT, ROWS),
            buf(FEAT, ROWS, dtype=F32), buf(FEAT, ROWS, dtype=F32),
            pltpu.SemaphoreType.DMA((N_SEM,)), pltpu.SemaphoreType.DMA((N_SEM,)),
            pltpu.SemaphoreType.DMA((N_LOCAL,)),
        ],
        compiler_params=pltpu.CompilerParams(
            collective_id=0, has_side_effects=True, vmem_limit_bytes=56 * 1024 * 1024
        ),
        name="step",
    )(tok, cot.T, ids, adv, lens, up.T, first.T, second.T, rows.T, down.T)
    new_weight, new_first, new_second, out = pl.pallas_call(
        hand_over,
        out_shape=out_shape,
        in_specs=[hbm, hbm, hbm, vmem],
        out_specs=(hbm, hbm, hbm, vmem),
        scratch_shapes=[
            buf(COLS, BLK), buf(COLS, BLK, dtype=F32), buf(COLS, BLK, dtype=F32),
            pltpu.SemaphoreType.DMA((12,)),
        ],
        name="hand_over",
    )(new_weight, new_first, new_second, out)
    return (new_weight.T, new_first.T, new_second.T, out)


def solution(mesh):
    torus = Mesh(mesh.devices.reshape(4, 2, 2, 8, 8), (Q, K, XH, Y, Z))
    in_specs = (
        P(None, REP),
        P(REP, COL),
        P(REP, None),
        P(REP, None),
        P(REP, None),
        P(REP, COL),
        P(REP, COL),
        P(REP, COL),
        P(REP, COL),
        P(None, COL),
    )
    out_specs = (P(REP, COL), P(REP, COL), P(REP, COL), P(COL, REP))
    step = jax.shard_map(body, mesh=torus, in_specs=in_specs, out_specs=out_specs, check_vma=False)

    def run(tokens, cot, ids, adv, up, first, second, rows, down, lengths):
        return step(tokens, cot, ids, adv, lengths, up, first, second, rows, down)

    return run
```

```python
import math

import jax
import jax.numpy as jnp
from jax import lax
from jax.experimental import pallas as pl
from jax.experimental.pallas import tpu as pltpu
from jax.sharding import Mesh
from jax.sharding import PartitionSpec as P

SEQS = 4
REP = ("rep_0", "rep_1")
COL = ("col_0", "col_1", "col_2")
Q, K, XH, Y, Z = "rep_0", "rep_1", "col_0", "col_1", "col_2"
MESH = pl.DeviceIdType.MESH
F32 = jnp.float32
BF16 = jnp.bfloat16

first_decay = 0.9
second_decay = 0.95
learn_rate = 0.003
decay_weight = 0.1
adam_epsilon = 1e-08
first_bias = 1.0 - math.exp(100.0 * math.log(0.9))
second_bias = 1.0 - math.exp(100.0 * math.log(0.95))

BLK = 640
COLS = 216
TOK = 256
ROWS = 128
FEAT = 40
HALF = 320
LIVE = 96
FOLD_COLS = 168
FOLD_HALF = 240
PIECES = ((0, 64), (64, 64), (128, 48), (176, 40))
RING = (4, 3, 5, 2, 6, 1, 7)

S_TOK, S_SC, S_R, S_L, S_X1 = 0, 4, 5, 21, 37
S_2A, S_2B, S_3A, S_3B, S_PRE = 39, 47, 55, 63, 71
S_1DA, S_1DB, S_2DA, S_2DB, S_XH = 79, 87, 95, 103, 111
N_SEM = 112
L_TOK, L_W, L_M, L_V, L_DN, L_OUT = 0, 4, 5, 6, 7, 8
N_LOCAL = 11


def adam_update(gradient, up_weight, first_moment, second_moment):
    new_first = first_decay * first_moment + (1.0 - first_decay) * gradient
    new_second = second_decay * second_moment + (1.0 - second_decay) * gradient * gradient
    direction = new_first / first_bias / (jnp.sqrt(new_second / second_bias) + adam_epsilon)
    weight_wide = up_weight.astype(F32)
    new_weight = (weight_wide - learn_rate * (direction + decay_weight * weight_wide)).astype(BF16)
    return (new_weight, new_first, new_second)


def fold(value, rows):
    quarter = value.shape[0] - rows
    tail = value[rows:]
    side = [pltpu.roll(tail, LIVE - 32 * s, 1) for s in range(3)]
    if 3 * quarter < rows:
        side.append(jnp.zeros((rows - 3 * quarter, ROWS), F32))
    lane = lax.broadcasted_iota(jnp.int32, (rows, ROWS), 1)
    return jnp.where(lane < LIVE, value[:rows], jnp.concatenate(side, axis=0))


def unfold(value, length):
    rows = value.shape[0]
    quarter = length - rows
    side = [pltpu.roll(value[s * quarter : (s + 1) * quarter], 32 + 32 * s, 1) for s in range(3)]
    lane = lax.broadcasted_iota(jnp.int32, (quarter, ROWS), 1)
    tail = jnp.where(lane < 32, side[0], jnp.where(lane < 64, side[1], side[2]))
    whole = jnp.concatenate([value, tail], axis=0)
    return jnp.where(lax.broadcasted_iota(jnp.int32, (length, ROWS), 1) < LIVE, whole, 0.0)


def picks(lens, dim):
    row = lax.broadcasted_iota(jnp.int32, (ROWS, ROWS), dim)
    place = lax.broadcasted_iota(jnp.int32, (ROWS, ROWS), 1 - dim)
    slot_len = ROWS // SEQS
    slot, within = row // slot_len, row % slot_len
    limit, ahead = jnp.zeros_like(row), jnp.zeros_like(row)
    before = jnp.int32(0)
    for s in range(SEQS):
        limit = jnp.where(slot == s, lens[0, s], limit)
        ahead = jnp.where(slot == s, before, ahead)
        before = before + lens[0, s]
    return jnp.where((within < limit) & (ahead + within == place), 1.0, 0.0).astype(BF16)


def kernel(
    tok, cot, ids, adv, lens, w_in, m_in, v_in, x_in, down,
    w_out, m_out, v_out, o_out,
    tok_a, tok_b, sc_o, sc_p, part, r_in, l_in, r_send, l_send,
    x_live, gath, p_send, p_recv,
    w_s, m_s, v_s, w_n, m_n, v_n, dn, dn_y, dn_z,
    a_send, a_recv, b_send, b_recv, sum_a, sum_b,
    a2_send, a2_recv, b2_send, b2_recv, x_send, x_recv,
    send, recv, local,
):
    q, k = lax.axis_index(Q), lax.axis_index(K)
    xh, y, z = lax.axis_index(XH), lax.axis_index(Y), lax.axis_index(Z)
    r = 2 * q + k

    def remote(src, dst, at_send, at_recv, where):
        return pltpu.make_async_remote_copy(
            src_ref=src,
            dst_ref=dst,
            send_sem=send.at[at_send],
            recv_sem=recv.at[at_recv],
            device_id=where,
            device_id_type=MESH,
        )

    leaving = []

    def send_to(src, dst, at_send, at_recv, where):
        copy = remote(src, dst, at_send, at_recv, where)
        copy.start()
        leaving.append(copy.wait_send)

    def arrived(dst, at_recv):
        remote(dst, dst, 0, at_recv, {K: 1 - k}).wait_recv()

    def sent(src, at_send):
        remote(src, src, at_send, 0, {K: 1 - k}).wait_send()

    barrier = pltpu.get_barrier_semaphore()

    def greet(where):
        pl.semaphore_signal(barrier, inc=1, device_id=where, device_id_type=MESH)

    from_q, from_k, from_x = y // 2, y % 2, q // 2
    from_y = [4 * (q % 2) + 2 * k + j for j in range(2)]
    mine_from = [(from_q == q) & (from_k == k) & (from_x == xh) & (from_y[j] == y) for j in range(2)]
    to_q, to_k = 2 * xh + y // 4, (y // 2) % 2
    mine_to = [(to_q == q) & (to_k == k) & (xh == h) & (r == y) for h in range(2)]

    for d in range(1, 8):
        other = (r + d) % 8
        greet({Q: other // 2, K: other % 2})
        greet({Y: (y + d) % 8})
        greet({Z: (z + d) % 8})
    greet({XH: 1 - xh})
    for j in range(2):

        @pl.when(jnp.logical_not(mine_from[j]))
        def _():
            greet({Q: from_q, K: from_k, XH: from_x, Y: from_y[j], Z: z})

    def block_rows(b, parity):
        return pl.ds(pl.multiple_of((2 * b + parity) * BLK, BLK), BLK)

    order = (3, 0, 2, 1)
    loads = [pltpu.make_async_copy(tok.at[block_rows(b, k)], tok_a.at[b], local.at[L_TOK + b]) for b in range(4)]
    for b in order:
        loads[b].start()
    late = [
        pltpu.make_async_copy(w_in, w_s, local.at[L_W]),
        pltpu.make_async_copy(m_in, m_s, local.at[L_M]),
        pltpu.make_async_copy(v_in, v_s, local.at[L_V]),
        pltpu.make_async_copy(down, dn, local.at[L_DN]),
    ]
    for copy in late:
        copy.start()

    x_live[...] = jnp.dot(x_in[...], picks(lens, 0), preferred_element_type=F32).astype(BF16)

    sample = lax.broadcasted_iota(jnp.int32, (8, TOK), 0)
    members = (ids[...] == sample).astype(F32)
    counts = jnp.sum(members, axis=1, keepdims=True)
    eye = lax.broadcasted_iota(jnp.int32, (8, 8), 0) == lax.broadcasted_iota(jnp.int32, (8, 8), 1)
    tall = jnp.sum(jnp.where(eye, adv[...], 0.0), axis=1, keepdims=True)
    scale = jnp.sum(members * (tall / counts), axis=0, keepdims=True)
    sc_o[...] = (scale * cot[...].astype(F32)).astype(BF16)

    pl.semaphore_wait(barrier, 24 - mine_to[0].astype(jnp.int32) - mine_to[1].astype(jnp.int32))

    for h in range(2):

        @pl.when(jnp.logical_not(mine_to[h]))
        def _():
            remote(x_live, gath.at[r, y % 2, z], S_X1 + h, S_X1 + y % 2, {Q: to_q, K: to_k, XH: h, Y: r, Z: z}).start()

        @pl.when(mine_to[h])
        def _():
            gath[r, y % 2, z] = x_live[...]

    send_to(sc_o, sc_p, S_SC, S_SC, {K: 1 - k})
    for b in order:
        send_to(tok.at[block_rows(b, 1 - k)], tok_b.at[b], S_TOK + b, S_TOK + b, {K: 1 - k})

    def running(b, s, first, sums, out, at, target):
        rows = pl.ds(*PIECES[s])
        value = part[b, rows]
        if not first:
            arrived(sums.at[b, rows], at + 4 * b + s)
            value = value + sums[b, rows].astype(F32)
        out[b, rows] = value.astype(BF16)
        remote(out.at[b, rows], sums.at[b, rows], at + 4 * b + s, at + 4 * b + s, {Q: target}).start()

    def right(b, s, first):
        running(b, s, first, r_in, r_send, S_R, q + 1)

    def left(b, s, first):
        running(b, s, first, l_in, l_send, S_L, q - 1)

    def over_tokens(scaled, tokens):
        return lax.dot_general(scaled, tokens, (((1,), (1,)), ((), ())), preferred_element_type=F32)

    def spread_rows():
        for j in range(2):

            @pl.when(jnp.logical_not(mine_from[j]))
            def _():
                arrived(gath.at[y, j, z], S_X1 + j)

        for d in RING:
            oz, oy = (z + d) % 8, (y + d) % 8
            here = gath.at[y, 0, z]
            send_to(here, here, S_2A + oz, S_2A + z, {Z: oz})
            here = gath.at[y, 1, z]
            send_to(here, here, S_2B + oy, S_2B + y, {Y: oy})

    arrived(sc_p, S_SC)
    for b in order:
        if b == order[-1]:
            spread_rows()
        loads[b].wait()
        arrived(tok_b.at[b], S_TOK + b)

        part[b] = over_tokens(sc_o[...], tok_a[b]) + over_tokens(sc_p[...], tok_b[b])

        if b > 0:

            @pl.when(q == 0)
            def _():
                for s in range(4):
                    right(b, s, True)

        if b < 3:

            @pl.when(q == 3)
            def _():
                for s in range(4):
                    left(b, s, True)

    @pl.when(q == 1)
    def _():
        for s in range(4):
            right(3, s, False)

    @pl.when(q == 2)
    def _():
        for s in range(4):
            left(0, s, False)

    for d in reversed(RING):
        oz = (z + d) % 8
        arrived(gath.at[y, 0, oz], S_2A + oz)
    for d in RING:
        oy = (y + d) % 8
        here = gath.at[y, 0]
        send_to(here, here, S_3A + oy, S_3A + y, {Y: oy})
    for d in reversed(RING):
        oy = (y + d) % 8
        arrived(gath.at[oy, 1, z], S_2B + oy)
    for d in RING:
        oz = (z + d) % 8
        here = gath.at[:, 1, z]
        send_to(here, here, S_3B + oz, S_3B + z, {Z: oz})

    @pl.when(q == 1)
    def _():
        for s in range(4):
            left(0, s, False)
        for s in range(4):
            right(2, s, False)

    @pl.when(q == 2)
    def _():
        for s in range(4):
            right(3, s, False)
        for s in range(4):
            left(1, s, False)

    late[3].wait()

    def turned(at):
        wide = jnp.concatenate([dn[:, at].astype(F32), jnp.zeros((256 - COLS, BLK), F32)], axis=0)
        return jnp.transpose(wide)[:, :COLS]

    @pl.loop(0, 4)
    def _(i):
        near = turned(pl.ds(pl.multiple_of(i * BLK, BLK), BLK)).astype(BF16)
        dn_y[2 * i] = near[:HALF]
        dn_y[2 * i + 1] = near[HALF:]
        far = turned(pl.ds(pl.multiple_of((4 + i) * BLK, BLK), BLK))
        for j in range(2):
            for n in range(8):
                at = j * HALF + n * FEAT
                dn_z[n, 2 * i + j] = far[at : at + FEAT].astype(BF16)

    @pl.when(q > 0)
    def _():
        for s in range(4):
            arrived(r_in.at[q, pl.ds(*PIECES[s])], S_R + 4 * q + s)

    @pl.when(q < 3)
    def _():
        for s in range(4):
            arrived(l_in.at[q, pl.ds(*PIECES[s])], S_L + 4 * q + s)

    for copy in late[:3]:
        copy.wait()
    has_left, has_right = q > 0, q < 3

    @pl.loop(0, 5)
    def _(i):
        lanes = pl.ds(pl.multiple_of(i * 128, 128), 128)
        for piece in PIECES:
            rows = pl.ds(*piece)
            gradient = part[q, rows, lanes]
            gradient = gradient + jnp.where(has_left, r_in[q, rows, lanes].astype(F32), 0.0)
            gradient = gradient + jnp.where(has_right, l_in[q, rows, lanes].astype(F32), 0.0)
            new = adam_update(gradient, w_s[rows, lanes], m_s[rows, lanes], v_s[rows, lanes])
            w_n[rows, lanes], m_n[rows, lanes], v_n[rows, lanes] = new

    outs = [
        pltpu.make_async_copy(w_n, w_out, local.at[L_OUT]),
        pltpu.make_async_copy(m_n, m_out, local.at[L_OUT + 1]),
        pltpu.make_async_copy(v_n, v_out, local.at[L_OUT + 2]),
    ]
    for copy in outs:
        copy.start()
        leaving.append(copy.wait)

    for d in RING:
        oy, oz = (y + d) % 8, (z + d) % 8
        arrived(gath.at[oy, 0], S_3A + oy)
        arrived(gath.at[:, 1, oz], S_3B + oz)

    def partial_of(other):
        return fold(jnp.dot(w_n[...], gath[other].reshape(BLK, ROWS), preferred_element_type=F32), FOLD_COLS)

    across = [(3 - q, k), (3 - q, 1 - k), ((q + 2) % 4, k), ((q + 2) % 4, 1 - k)]
    beside = q + 1 - 2 * (q % 2)
    for oq, ok in across + [(beside, k), (beside, 1 - k), (q, 1 - k)]:
        other = 2 * oq + ok
        p_send[other] = partial_of(other).astype(BF16)
        send_to(p_send.at[other], p_recv.at[r], S_PRE + other, S_PRE + r, {Q: oq, K: ok})
    pre = partial_of(r)
    for d in range(1, 8):
        other = (r + d) % 8
        arrived(p_recv.at[other], S_PRE + other)
        pre = pre + p_recv[other].astype(F32)

    pre = unfold(pre, COLS)
    act = (pre / (1.0 + jnp.exp(-pre))).astype(BF16)

    def down_y(oy):
        return fold(jnp.dot(dn_y[oy], act, preferred_element_type=F32), FOLD_HALF)

    def down_z(oz):
        return fold(jnp.dot(dn_z[oz].reshape(HALF, COLS), act, preferred_element_type=F32), FOLD_HALF)

    for d in RING:
        oy, oz = (y + d) % 8, (z + d) % 8
        a_send[oy] = down_y(oy).astype(BF16)
        send_to(a_send.at[oy], a_recv.at[y], S_1DA + oy, S_1DA + y, {Y: oy})
        b_send[oz] = down_z(oz).astype(BF16)
        send_to(b_send.at[oz], b_recv.at[z], S_1DB + oz, S_1DB + z, {Z: oz})
    own_a, own_b = down_y(y), down_z(z)

    value = own_a
    for d in RING:
        oy = (y + d) % 8
        arrived(a_recv.at[oy], S_1DA + oy)
        value = value + a_recv[oy].astype(F32)
    sum_a[...] = unfold(value, HALF)
    for d in RING:
        oz = (z + d) % 8
        a2_send[oz] = sum_a[pl.ds(pl.multiple_of(oz * FEAT, 8), FEAT)].astype(BF16)
        send_to(a2_send.at[oz], a2_recv.at[z], S_2DA + oz, S_2DA + z, {Z: oz})

    value = own_b
    for d in RING:
        oz = (z + d) % 8
        arrived(b_recv.at[oz], S_1DB + oz)
        value = value + b_recv[oz].astype(F32)
    sum_b[...] = unfold(value, HALF)
    for d in RING:
        oy = (y + d) % 8
        b2_send[oy] = sum_b[pl.ds(pl.multiple_of(oy * FEAT, 8), FEAT)].astype(BF16)
        send_to(b2_send.at[oy], b2_recv.at[y], S_2DB + oy, S_2DB + y, {Y: oy})

    res_a = sum_a[pl.ds(pl.multiple_of(z * FEAT, 8), FEAT)]
    for d in RING:
        oz = (z + d) % 8
        arrived(a2_recv.at[oz], S_2DA + oz)
        res_a = res_a + a2_recv[oz].astype(F32)
    res_b = sum_b[pl.ds(pl.multiple_of(y * FEAT, 8), FEAT)]
    for d in RING:
        oy = (y + d) % 8
        arrived(b2_recv.at[oy], S_2DB + oy)
        res_b = res_b + b2_recv[oy].astype(F32)

    x_send[...] = jnp.where(xh == 0, res_b, res_a).astype(BF16)
    send_to(x_send, x_recv, S_XH, S_XH, {XH: 1 - xh})
    arrived(x_recv, S_XH)
    total = (jnp.where(xh == 0, res_a, res_b) + x_recv[...].astype(F32)).astype(BF16)
    o_out[...] = jnp.dot(total, picks(lens, 1), preferred_element_type=F32).astype(BF16)

    for wait in leaving:
        wait()
    for b in range(4):
        for s in range(4):
            rows = pl.ds(*PIECES[s])

            @pl.when(q < b)
            def _():
                sent(r_send.at[b, rows], S_R + 4 * b + s)

            @pl.when(q > b)
            def _():
                sent(l_send.at[b, rows], S_L + 4 * b + s)

    for h in range(2):

        @pl.when(jnp.logical_not(mine_to[h]))
        def _():
            sent(x_live, S_X1 + h)


def hand_over(*refs):
    given, kept, held, sems = refs[:4], refs[4:8], refs[8:12], refs[12]
    cuts = [(n, 0, 112) for n in range(3)] + [(n, 112, COLS - 112) for n in range(3)] + [(3, 0, FEAT)]
    into, back = [], []
    for i, (n, start, size) in enumerate(cuts):
        rows = pl.ds(start, size)
        into.append(pltpu.make_async_copy(given[n].at[rows], held[n].at[rows], sems.at[2 * i]))
        back.append(pltpu.make_async_copy(held[n].at[rows], kept[n].at[rows], sems.at[2 * i + 1]))
    for copy in into:
        copy.start()
    for first, second in zip(into, back):
        first.wait()
        second.start()
    for copy in back:
        copy.wait()


def body(tok, cot, ids, adv, lens, up, first, second, rows, down):
    vmem, hbm, smem = (
        pl.BlockSpec(memory_space=pltpu.VMEM),
        pl.BlockSpec(memory_space=pl.ANY),
        pl.BlockSpec(memory_space=pltpu.SMEM),
    )

    def buf(*shape, dtype=BF16):
        return pltpu.VMEM(shape, dtype)

    out_shape = (
        jax.ShapeDtypeStruct((COLS, BLK), BF16),
        jax.ShapeDtypeStruct((COLS, BLK), F32),
        jax.ShapeDtypeStruct((COLS, BLK), F32),
        jax.ShapeDtypeStruct((FEAT, ROWS), BF16),
    )
    new_weight, new_first, new_second, out = pl.pallas_call(
        kernel,
        out_shape=out_shape,
        in_specs=[hbm, vmem, vmem, vmem, smem, hbm, hbm, hbm, vmem, hbm],
        out_specs=(hbm, hbm, hbm, vmem),
        scratch_shapes=[
            buf(4, BLK, TOK), buf(4, BLK, TOK), buf(COLS, TOK), buf(COLS, TOK),
            buf(4, COLS, BLK, dtype=F32),
            buf(4, COLS, BLK), buf(4, COLS, BLK), buf(4, COLS, BLK), buf(4, COLS, BLK),
            buf(FEAT, ROWS), buf(8, 2, 8, FEAT, ROWS), buf(8, FOLD_COLS, ROWS), buf(8, FOLD_COLS, ROWS),
            buf(COLS, BLK), buf(COLS, BLK, dtype=F32), buf(COLS, BLK, dtype=F32),
            buf(COLS, BLK), buf(COLS, BLK, dtype=F32), buf(COLS, BLK, dtype=F32),
            buf(COLS, 8 * BLK), buf(8, HALF, COLS), buf(8, 8, FEAT, COLS),
            buf(8, FOLD_HALF, ROWS), buf(8, FOLD_HALF, ROWS), buf(8, FOLD_HALF, ROWS), buf(8, FOLD_HALF, ROWS),
            buf(HALF, ROWS, dtype=F32), buf(HALF, ROWS, dtype=F32),
            buf(8, FEAT, ROWS), buf(8, FEAT, ROWS), buf(8, FEAT, ROWS), buf(8, FEAT, ROWS),
            buf(FEAT, ROWS), buf(FEAT, ROWS),
            pltpu.SemaphoreType.DMA((N_SEM,)), pltpu.SemaphoreType.DMA((N_SEM,)),
            pltpu.SemaphoreType.DMA((N_LOCAL,)),
        ],
        compiler_params=pltpu.CompilerParams(
            collective_id=0, has_side_effects=True, vmem_limit_bytes=56 * 1024 * 1024
        ),
        name="step",
    )(tok, cot.T, ids, adv, lens, up.T, first.T, second.T, rows.T, down.T)
    new_weight, new_first, new_second, out = pl.pallas_call(
        hand_over,
        out_shape=out_shape,
        in_specs=[hbm, hbm, hbm, hbm],
        out_specs=(hbm, hbm, hbm, hbm),
        scratch_shapes=[
            buf(COLS, BLK), buf(COLS, BLK, dtype=F32), buf(COLS, BLK, dtype=F32), buf(FEAT, ROWS),
            pltpu.SemaphoreType.DMA((14,)),
        ],
        name="hand_over",
    )(new_weight, new_first, new_second, out)
    return (new_weight.T, new_first.T, new_second.T, out)


def solution(mesh):
    torus = Mesh(mesh.devices.reshape(4, 2, 2, 8, 8), (Q, K, XH, Y, Z))
    in_specs = (
        P(None, REP),
        P(REP, COL),
        P(REP, None),
        P(REP, None),
        P(REP, None),
        P(REP, COL),
        P(REP, COL),
        P(REP, COL),
        P(REP, COL),
        P(None, COL),
    )
    out_specs = (P(REP, COL), P(REP, COL), P(REP, COL), P(COL, REP))
    step = jax.shard_map(body, mesh=torus, in_specs=in_specs, out_specs=out_specs, check_vma=False)

    def run(tokens, cot, ids, adv, up, first, second, rows, down, lengths):
        return step(tokens, cot, ids, adv, lengths, up, first, second, rows, down)

    return run
```
